512 devices in a mesh: grp: 16 (over z_lo, x), blk: 32 (over y, z_hi, core).
Axes of the slice: x: 4, y: 8, z: 8 (z_hi: 2, z_lo: 4; z = z_hi * 4 + z_lo), core: 2. Of those that a mesh axis runs over, the one named last changes fastest.
Arguments:
- queries: bfloat16 [65536, 4096], P(('grp', 'blk')), may hold values from -4 to 4
- passages: bfloat16 [65536, 4096], P(('grp', 'blk')), may hold values from -1 to 1
- hard_index: int32 [65536, 3], P(('grp', 'blk')), may hold values from 0 to 65535, as said below
- weights: float32 [65536], P(('grp', 'blk')), may hold values from 0.5 to 2
Outputs:
- loss_rows: float32 [65536], P(('grp', 'blk'))
- grad_queries: bfloat16 [65536, 4096], P(('grp', 'blk'))
- grad_passages: bfloat16 [65536, 4096], P(('grp', 'blk'))
The draws below stay inside these ranges and needn't reach their ends.
Inputs may be any that keep to these rules, and one draw needn't show every extreme that they name: `hard_index`: the three entries of query i name passages of the block at the same index of blk as query i in three different groups, none its own; among the queries of one device at most 26 entries name one group, and in every device exactly 26 entries name some group.
All inputs are finite; a program needn't handle non-finite values.
Results may differ from the reference program's by a relative error of at most 0.0065.
Values may be sent and summed in bfloat16 or wider, within the bound.
A program may use at most 64 MiB of HBM per device.

```python
import math
import jax
import jax.numpy as jnp
from jax import lax

D = 4096
ROWS = 128
WINDOW = 4
GROUPS = 16
LOOP = 32
TOTAL = 65536
CAP = 26


def base_passages(key):
    total_rows = GROUPS * LOOP * ROWS
    raw_values = jax.random.normal(jax.random.fold_in(key, 11), (total_rows, D), jnp.float32) * D ** (-0.5)
    return jnp.clip(raw_values, -1.0, 1.0)


def hard_targets(key):
    blocks = GROUPS * LOOP
    others = GROUPS - 1

    def per_block(block_key, block_id):
        key_order = jax.random.fold_in(block_key, 1)
        key_rows = jax.random.fold_in(block_key, 2)
        order = jax.random.permutation(key_order, others)
        position = (jnp.arange(3)[None, :] * ROWS + jnp.arange(ROWS)[:, None]) // CAP
        offset = order[position]
        group_id = block_id // LOOP
        blk_id = block_id % LOOP
        target_group = (group_id + 1 + offset) % GROUPS
        row_pick = jax.random.randint(key_rows, (ROWS, 3), 0, ROWS)
        return ((target_group * LOOP + blk_id) * ROWS + row_pick).astype(jnp.int32)
    block_keys = jax.random.split(jax.random.fold_in(key, 7), blocks)
    return jax.vmap(per_block)(block_keys, jnp.arange(blocks)).reshape(blocks * ROWS, 3)


def draw_passages(key, part):
    return base_passages(key).astype(jnp.bfloat16)


def draw_hard_index(key, part):
    return hard_targets(key)


def draw_queries(key, part):
    total_rows = GROUPS * LOOP * ROWS
    group_rows = LOOP * ROWS
    base_rows = base_passages(key)
    targets = hard_targets(key)
    group_keys = jax.random.split(jax.random.fold_in(key, 13), GROUPS)
    partner_rows = jax.vmap(lambda group_key: jax.random.permutation(group_key, group_rows))(group_keys)
    partner_rows = (partner_rows + jnp.arange(GROUPS)[:, None] * group_rows).reshape(total_rows)
    noise_part = jax.random.normal(jax.random.fold_in(key, 15), (total_rows, D), jnp.float32) * D ** (-0.5)
    mixture = 0.12 * base_rows + 0.1 * (base_rows[targets[:, 0]] + base_rows[targets[:, 1]] + base_rows[targets[:, 2]])
    mixture = mixture + 0.1 * base_rows[partner_rows] + 0.9 * noise_part
    return jnp.clip(mixture, -4.0, 4.0).astype(jnp.bfloat16)


def block_scale(own_key, shape, cuts, smallest, top_value):
    loudness, own = 1.0, jax.random.fold_in(own_key, 6)
    for dim, blocks in cuts:
        draws = jnp.exp(jax.random.uniform(jax.random.fold_in(own, dim), (blocks,), jnp.float32, smallest / len(cuts), top_value / len(cuts)))
        loudness = loudness * jnp.repeat(draws, shape[dim] // blocks).reshape([-1 if axis == dim else 1 for axis in range(len(shape))])
    return loudness


def setup_inputs(seed: int = 0) -> dict:
    arg_keys = jax.random.split(jax.random.key(seed), 5)
    return {
        "queries": draw_queries(jax.random.fold_in(arg_keys[4], 71), 0),
        "passages": draw_passages(jax.random.fold_in(arg_keys[4], 71), 0),
        "hard_index": draw_hard_index(jax.random.fold_in(arg_keys[4], 71), 0),
        "weights": jnp.clip(jnp.exp(math.log(2.0) - 1.3862944 * jax.random.uniform(arg_keys[3], (TOTAL,), jnp.float32) ** block_scale(arg_keys[3], (TOTAL,), ((0, 512),), -0.2, 0.2)), 0.5, 2.0),
    }


def reference(queries, passages, hard_index, weights):
    block_total = GROUPS * LOOP
    q_blocks = queries.reshape(block_total, ROWS, D)
    p_blocks = passages.reshape(block_total, ROWS, D)
    index_blocks = hard_index.reshape(block_total, ROWS, 3)
    weight_blocks = weights.reshape(block_total, ROWS)

    def first(hard_extra, block_id):
        group_id = block_id // LOOP
        blk_id = block_id % LOOP
        q_here = q_blocks[block_id]
        weight_here = weight_blocks[block_id]
        index_here = index_blocks[block_id]
        window = jnp.concatenate([p_blocks[group_id * LOOP + (blk_id + s) % LOOP] for s in range(WINDOW)], axis=0)
        hard_rows = passages[index_here.reshape(-1)].reshape(ROWS, 3, D)
        scores = 50.0 * jnp.dot(q_here, window.T, preferred_element_type=jnp.float32)
        hard_scores = 50.0 * jnp.einsum("rd,rkd->rk", q_here.astype(jnp.float32), hard_rows.astype(jnp.float32))
        largest = jnp.maximum(jnp.max(scores, axis=1), jnp.max(hard_scores, axis=1))
        summed = jnp.sum(jnp.exp(scores - largest[:, None]), axis=1) + jnp.sum(jnp.exp(hard_scores - largest[:, None]), axis=1)
        log_total = largest + jnp.log(summed)
        loss_part = log_total - jnp.diagonal(scores[:, :ROWS])
        weight_col = weight_here[:, None]
        weighting = (weight_col * jnp.exp(scores - log_total[:, None])).astype(jnp.bfloat16)
        hard_weighting = (weight_col * jnp.exp(hard_scores - log_total[:, None])).astype(jnp.bfloat16)
        pulled = jnp.dot(weighting, window, preferred_element_type=jnp.float32)
        pulled = pulled + jnp.einsum("rk,rkd->rd", hard_weighting.astype(jnp.float32), hard_rows.astype(jnp.float32))
        grad_q = (50.0 * (pulled - weight_col * p_blocks[block_id].astype(jnp.float32))).astype(jnp.bfloat16)
        terms = (hard_weighting.astype(jnp.float32)[:, :, None] * q_here.astype(jnp.float32)[:, None, :]).astype(jnp.bfloat16)
        terms = lax.optimization_barrier(terms).astype(jnp.float32)
        hard_extra = hard_extra.at[index_here.reshape(-1)].add(terms.reshape(-1, D))
        return hard_extra, (loss_part, grad_q, weighting)

    start_extra = jnp.zeros((block_total * ROWS, D), jnp.float32)
    block_ids = jnp.arange(block_total).astype(jnp.int32)
    hard_extra, (loss_rows, grad_q, weighting_all) = lax.scan(first, start_extra, block_ids)

    def second(carry, block_id):
        group_id = block_id // LOOP
        blk_id = block_id % LOOP
        total = -weight_blocks[block_id][:, None] * q_blocks[block_id].astype(jnp.float32)
        for s in range(WINDOW):
            source = group_id * LOOP + (blk_id - s) % LOOP
            coef = weighting_all[source][:, s * ROWS:(s + 1) * ROWS]
            total = total + jnp.dot(coef.T, q_blocks[source], preferred_element_type=jnp.float32)
        return carry, total

    unused, in_group = lax.scan(second, jnp.zeros((), jnp.float32), block_ids)
    grad_passages = (50.0 * (in_group.reshape(-1, D) + hard_extra)).astype(jnp.bfloat16)
    return loss_rows.reshape(-1), grad_q.reshape(-1, D), grad_passages
```

```python
import functools

import jax
import jax.numpy as jnp
from jax import lax
from jax.experimental import pallas as pl
from jax.experimental.pallas import tpu as pltpu
from jax.sharding import PartitionSpec as P

MESH = pl.DeviceIdType.MESH
TEMP = 50.0
SLOTS = 32
NEG = -3.0e38
F32, BF16 = jnp.float32, jnp.bfloat16


def nt(a, b):
    return lax.dot_general(a, b, (((1,), (1,)), ((), ())), preferred_element_type=F32)


def tn(a, b):
    return lax.dot_general(a, b, (((0,), (0,)), ((), ())), preferred_element_type=F32)


def nn(a, b):
    return lax.dot_general(a, b, (((1,), (0,)), ((), ())), preferred_element_type=F32)


def kernel(
    NC, Y, q_hbm, p_hbm, rt, st, mc, mx, wcol, loss, gq_hbm, gp_hbm,
    col, bw, tr, xs, xr, rx, sc, acc, wts, mts, wtw, wtc, mtx, oq, op,
    ld_s, st_s, z_s, col_r, tr_r, own_s, win_s, bw_r, x_s, x_r,
    rx_s, rx_r, sc_s, sc_r, ww_s, ww_r, wc_s, wc_r, mt_s, mt_r,
):
    rows = 128
    dc = gq_hbm.shape[1] // NC
    g = lax.axis_index("grp")
    b = lax.axis_index("blk")
    p, x = g // 4, g % 4
    y, h, c = b // 4, (b // 2) % 2, b % 2
    z = h * 4 + p
    loop = 4 * Y
    m = p // 2
    outer = (p == 0) | (p == 3)

    def a(k):
        return k + m * (3 - 2 * k)

    def zdev(zz):
        zz = (zz + 8) % 8
        return ((zz % 4) * 4 + x, y * 4 + (zz // 4) * 2 + c)

    def ydev(yy, cc):
        return (g, ((yy + Y) % Y) * 4 + h * 2 + cc)

    def bdev(off):
        return (g, (b + off + loop) % loop)

    def xdev(xx, pp):
        return (pp * 4 + xx, b)

    z_in, z_out = zdev(z + 1 - 2 * m), zdev(z - 1 + 2 * m)

    def rcopy(src, dst, ssem, rsem, dev):
        return pltpu.make_async_remote_copy(
            src_ref=src, dst_ref=dst, send_sem=ssem, recv_sem=rsem, device_id=dev, device_id_type=MESH
        )

    def got(ref, rsem):
        rcopy(ref, ref, rsem, rsem, bdev(1)).wait_recv()

    def sent(ref, ssem):
        rcopy(ref, ref, ssem, ssem, bdev(1)).wait_send()

    barrier = pltpu.get_barrier_semaphore()

    def hello(dev):
        pl.semaphore_signal(barrier, inc=1, device_id=dev, device_id_type=MESH)

    for k in range(1, 16):
        hello(((g + k) % 16, b))
    for off in (1, 2, 3, 4):
        hello(bdev(off))
        hello(bdev(-off))
    hello(bdev(5 - 10 * c))

    @pl.when(outer)
    def _():
        hello(z_out)

    def load(src, i, cc):
        return pltpu.make_async_copy(
            src.at[:, pl.ds(pl.multiple_of(cc * dc, dc), dc)], col.at[p, cc, i], ld_s.at[i, cc]
        )

    def start_load(cc, carry):
        load(p_hbm, 0, cc).start()
        load(q_hbm, 1, cc).start()
        return carry

    lax.fori_loop(0, NC, start_load, 0)

    pl.semaphore_wait(barrier, 25 - ((p + 1) // 2) % 2)

    for dx in (1, 2, 3):
        xd = (x + dx) % 4
        rcopy(rt.at[:, xd], rx.at[:, x], rx_s.at[dx - 1], rx_r.at[x], xdev(xd, p)).start()
        pd = (p + dx) % 4
        rcopy(st.at[pd], sc.at[p], sc_s.at[dx - 1], sc_r.at[p], xdev(x, pd)).start()
    rx[:, x] = jnp.zeros((4, SLOTS, rows), BF16)
    sc[p] = st[p]

    def own(cc):
        load(p_hbm, 0, cc).wait()
        load(q_hbm, 1, cc).wait()
        src = col.at[p, cc]
        rcopy(src, col.at[p, cc], z_s.at[0, cc], col_r.at[p, cc], z_in).start()

        @pl.when(jnp.logical_not(outer))
        def _():
            rcopy(src, col.at[p, cc], z_s.at[1, cc], col_r.at[p, cc], z_out).start()

        pdst = 2 - 2 * c
        rcopy(col.at[p, cc, 0], bw.at[pdst, cc], own_s.at[0, cc], bw_r.at[pdst, cc], ydev(y - 1 + c, 1 - c)).start()
        qdst = 3 + 2 * c
        rcopy(col.at[p, cc, 1], bw.at[qdst, cc], own_s.at[1, cc], bw_r.at[qdst, cc], ydev(y + c, 1 - c)).start()

    def fwd_col(l, cc, k, dev):
        got(col.at[l, cc], col_r.at[l, cc])
        rcopy(col.at[l, cc], col.at[l, cc], z_s.at[k, cc], col_r.at[l, cc], dev).start()

    def to_win(src, cc, k, dev, hh):
        pi, qi = 1 + 5 * hh, 6 - 2 * hh
        rcopy(src.at[0], bw.at[pi, cc], z_s.at[k, cc], bw_r.at[pi, cc], dev).start()
        rcopy(src.at[1], bw.at[qi, cc], z_s.at[k + 1, cc], bw_r.at[qi, cc], dev).start()

    def hop12(cc):
        @pl.when(outer)
        def _():
            got(col.at[a(2), cc], col_r.at[a(2), cc])
            rcopy(col.at[a(2), cc], tr.at[cc], z_s.at[2, cc], tr_r.at[cc], z_out).start()

        @pl.when(jnp.logical_not(outer))
        def _():
            fwd_col(a(0), cc, 2, z_in)
            fwd_col(a(2), cc, 3, z_out)
            fwd_col(a(3), cc, 4, z_out)

    def hop3(cc):
        @pl.when(outer)
        def _():
            got(col.at[a(3), cc], col_r.at[a(3), cc])
            to_win(col.at[a(3), cc], cc, 3, z_out, 1 - h)
            got(tr.at[cc], tr_r.at[cc])
            to_win(tr.at[cc], cc, 5, z_in, h)
            got(col.at[a(1), cc], col_r.at[a(1), cc])

    def win(cc):
        wi = 1 + 3 * h
        got(bw.at[wi, cc], bw_r.at[wi, cc])
        d = h * (5 - 2 * c) + (1 - h) * 2 * c
        rcopy(bw.at[wi, cc], bw.at[d, cc], win_s.at[0, cc], bw_r.at[d, cc], ydev(y, 1 - c)).start()
        got(bw.at[6, cc], bw_r.at[6, cc])
        for c2 in (0, 1):
            d = h * (1 - c2 + c) + (1 - h) * (4 + c2 - c)
            rcopy(
                bw.at[6, cc], bw.at[d, cc], win_s.at[1 + c2, cc], bw_r.at[d, cc], ydev(y + 1 - 2 * h, c2)
            ).start()

    def pick(cc):
        for l in range(4):
            rows_p = nn(rx[l].reshape(4 * SLOTS, rows), col[l, cc, 0]).astype(BF16)
            xs[:, cc, 0, l * SLOTS : (l + 1) * SLOTS, :] = rows_p.reshape(4, SLOTS, dc)
            rows_q = nn(sc[l].reshape(4 * SLOTS, rows), col[l, cc, 1]).astype(BF16)
            xs[:, cc, 1, l * SLOTS : (l + 1) * SLOTS, :] = rows_q.reshape(4, SLOTS, dc)
        for dx in (2, 1, 3):
            xd = (x + dx) % 4
            rcopy(xs.at[xd, cc], xr.at[x, cc], x_s.at[dx - 1, cc], x_r.at[x, cc], xdev(xd, p)).start()

    own(0)
    own(1)
    for dx in (1, 2, 3):
        got(rx.at[:, (x + dx) % 4], rx_r.at[(x + dx) % 4])
        got(sc.at[(p + dx) % 4], sc_r.at[(p + dx) % 4])

    def step(t, carry):
        @pl.when(t < NC)
        def _():
            @pl.when(t + 2 < NC)
            def _():
                own(t + 2)

            hop12(t)

        @pl.when((t >= 1) & (t < NC + 1))
        def _():
            hop3(t - 1)
            pick(t - 1)

        @pl.when(t >= 2)
        def _():
            win(t - 2)

        return carry

    lax.fori_loop(0, NC + 2, step, 0)

    acc[...] = jnp.zeros_like(acc)

    def score(cc, carry):
        for i in (0, 2, 3, 5):
            got(bw.at[i, cc], bw_r.at[i, cc])
        got(bw.at[4 - 3 * h, cc], bw_r.at[4 - 3 * h, cc])
        for dx in (1, 2, 3):
            got(xr.at[(x + dx) % 4, cc], x_r.at[(x + dx) % 4, cc])
        q = col[p, cc, 1]
        acc[0] += nt(q, col[p, cc, 0])
        for s in range(3):
            acc[1 + s] += nt(q, bw[s, cc])
            acc[4 + s] += nt(q, col[(p + 1 + s) % 4, cc, 0])
            acc[7 + s] += nt(q, xr[(x + 1 + s) % 4, cc, 0])
        return carry

    lax.fori_loop(0, NC, score, 0)

    w = wcol[...]
    masks = [mc[(p + 1 + s) % 4] for s in range(3)] + [mx[(x + 1 + s) % 4] for s in range(3)]
    scores = [TEMP * acc[k] for k in range(4)]
    scores += [jnp.where(masks[k] > 0.5, TEMP * acc[4 + k], NEG) for k in range(6)]
    top = scores[0]
    for k in range(1, 10):
        top = jnp.maximum(top, scores[k])
    top = jnp.max(top, axis=1, keepdims=True)
    total = jnp.zeros((rows, rows), F32)
    for k in range(10):
        e = jnp.exp(scores[k] - top)
        total += e if k < 4 else jnp.where(masks[k - 4] > 0.5, e, 0.0)
    log_total = top + jnp.log(jnp.sum(total, axis=1, keepdims=True))
    ri = lax.broadcasted_iota(jnp.int32, (rows, rows), 0)
    ci = lax.broadcasted_iota(jnp.int32, (rows, rows), 1)
    loss[...] = jnp.sum(jnp.where(ri == ci, log_total - scores[0], 0.0), axis=0, keepdims=True)
    for k in range(10):
        e = w * jnp.exp(scores[k] - log_total)
        wts[k] = (e if k < 4 else jnp.where(masks[k - 4] > 0.5, e, 0.0)).astype(BF16)
    ones = jnp.ones((rows, rows), BF16)
    for s in range(3):
        xd = (x + 1 + s) % 4
        by_slot = tn(wts[7 + s], ones)
        mts[s] = (by_slot * rt[:, xd].reshape(rows, rows).astype(F32)).astype(BF16).reshape(4, SLOTS, rows)

    for s in range(3):
        rcopy(wts.at[1 + s], wtw.at[s], ww_s.at[s], ww_r.at[s], bdev(1 + s)).start()
        pd = (p + 1 + s) % 4
        rcopy(wts.at[4 + s], wtc.at[p], wc_s.at[s], wc_r.at[p], xdev(x, pd)).start()
        xd = (x + 1 + s) % 4
        for l in range(4):
            rcopy(mts.at[s, l], mtx.at[x, p], mt_s.at[s, l], mt_r.at[x, p], xdev(xd, l)).start()

    def store(src, dst, i, cc):
        return pltpu.make_async_copy(
            src.at[cc], dst.at[:, pl.ds(pl.multiple_of(cc * dc, dc), dc)], st_s.at[i, cc]
        )

    def queries(cc, carry):
        own_p = col[p, cc, 0]
        tot = nn(wts[0], own_p)
        for s in range(3):
            tot += nn(wts[1 + s], bw[s, cc])
            tot += nn(wts[4 + s], col[(p + 1 + s) % 4, cc, 0])
            tot += nn(wts[7 + s], xr[(x + 1 + s) % 4, cc, 0])
        oq[cc] = (TEMP * (tot - w * own_p.astype(F32))).astype(BF16)
        store(oq, gq_hbm, 0, cc).start()
        return carry

    lax.fori_loop(0, NC, queries, 0)

    for s in range(3):
        got(wtw.at[s], ww_r.at[s])
        pd, xd = (p + 1 + s) % 4, (x + 1 + s) % 4
        got(wtc.at[pd], wc_r.at[pd])
        for l in range(4):
            got(mtx.at[xd, l], mt_r.at[xd, l])

    def passages(cc, carry):
        own_q = col[p, cc, 1]
        tot = tn(wts[0], own_q)
        for s in range(3):
            tot += tn(wtw[s], bw[3 + s, cc])
            pd, xd = (p + 1 + s) % 4, (x + 1 + s) % 4
            tot += tn(wtc[pd], col[pd, cc, 1])
            tot += tn(mtx[xd].reshape(rows, rows), xr[xd, cc, 1])
        op[cc] = (TEMP * (tot - w * own_q.astype(F32))).astype(BF16)
        store(op, gp_hbm, 1, cc).start()
        return carry

    lax.fori_loop(0, NC, passages, 0)

    def drain(cc, carry):
        store(oq, gq_hbm, 0, cc).wait()
        store(op, gp_hbm, 1, cc).wait()
        sent(col.at[p, cc], z_s.at[0, cc])
        sent(col.at[p, cc, 0], own_s.at[0, cc])
        sent(col.at[p, cc, 1], own_s.at[1, cc])
        sent(col.at[p, cc], z_s.at[2, cc])
        for k in range(3):
            sent(bw.at[6, cc], win_s.at[k, cc])
            sent(xs.at[0, cc], x_s.at[k, cc])

        @pl.when(outer)
        def _():
            for k in (3, 4, 5, 6):
                sent(col.at[p, cc, 0], z_s.at[k, cc])

        @pl.when(jnp.logical_not(outer))
        def _():
            for k in (1, 3, 4):
                sent(col.at[p, cc], z_s.at[k, cc])

        return carry

    lax.fori_loop(0, NC, drain, 0)
    for s in range(3):
        sent(rt.at[:, 0], rx_s.at[s])
        sent(st.at[0], sc_s.at[s])
        sent(wts.at[1 + s], ww_s.at[s])
        sent(wts.at[4 + s], wc_s.at[s])
        for l in range(4):
            sent(mts.at[s, l], mt_s.at[s, l])


def index_tiles(hard_index, x, rows, loop):
    target = hard_index // (loop * rows)
    wanted = hard_index % rows
    hit = target[:, :, None] == jnp.arange(16)[None, None, :]
    named = jnp.any(hit, axis=1).astype(F32)
    row = jnp.sum(jnp.where(hit, wanted[:, :, None], 0), axis=1)
    before = (jnp.arange(rows)[:, None] > jnp.arange(rows)[None, :]).astype(F32)
    rank = jnp.dot(before, named, preferred_element_type=F32).astype(jnp.int32)
    rank = jnp.where(named > 0, rank, -1)
    picks = rank.T[:, None, :] == jnp.arange(SLOTS)[None, :, None]
    slot_row = jnp.max(jnp.where(picks, row.T[:, None, :], -1), axis=2)
    st = picks.astype(BF16).reshape(4, 4, SLOTS, rows)
    rt = (slot_row[:, :, None] == jnp.arange(rows)[None, None, :]).astype(BF16).reshape(4, 4, SLOTS, rows)
    lanes = jnp.arange(rows)
    rank4 = rank.reshape(rows, 4, 4).transpose(2, 0, 1)
    lane_rank = jnp.repeat(rank4, SLOTS, axis=2)
    mx = (lane_rank == (lanes % SLOTS)[None, None, :]).astype(F32)
    col_id = jnp.arange(4) * 4 + x
    mc = jnp.any(
        (target[None, :, :, None] == col_id[:, None, None, None]) & (wanted[None, :, :, None] == lanes), axis=2
    ).astype(F32)
    return rt, st, mc, mx


def per_device(NC, Y, queries, passages, hard_index, weights):
    rows, width = queries.shape
    loop = 4 * Y
    x = lax.axis_index("grp") % 4
    rt, st, mc, mx = index_tiles(hard_index, x, rows, loop)
    dc = width // NC
    dma = pltpu.SemaphoreType.DMA
    vmem = pl.BlockSpec(memory_space=pltpu.VMEM)
    hbm = pl.BlockSpec(memory_space=pl.ANY)
    loss, gq, gp = pl.pallas_call(
        functools.partial(kernel, NC, Y),
        out_shape=(
            jax.ShapeDtypeStruct((1, rows), F32),
            jax.ShapeDtypeStruct((rows, width), BF16),
            jax.ShapeDtypeStruct((rows, width), BF16),
        ),
        in_specs=[hbm, hbm, vmem, vmem, vmem, vmem, vmem],
        out_specs=(vmem, hbm, hbm),
        scratch_shapes=[
            pltpu.VMEM((4, NC, 2, rows, dc), BF16),
            pltpu.VMEM((7, NC, rows, dc), BF16),
            pltpu.VMEM((NC, 2, rows, dc), BF16),
            pltpu.VMEM((4, NC, 2, rows, dc), BF16),
            pltpu.VMEM((4, NC, 2, rows, dc), BF16),
            pltpu.VMEM((4, 4, SLOTS, rows), BF16),
            pltpu.VMEM((4, 4, SLOTS, rows), BF16),
            pltpu.VMEM((10, rows, rows), F32),
            pltpu.VMEM((10, rows, rows), BF16),
            pltpu.VMEM((3, 4, SLOTS, rows), BF16),
            pltpu.VMEM((3, rows, rows), BF16),
            pltpu.VMEM((4, rows, rows), BF16),
            pltpu.VMEM((4, 4, SLOTS, rows), BF16),
            pltpu.VMEM((NC, rows, dc), BF16),
            pltpu.VMEM((NC, rows, dc), BF16),
            dma((2, NC)),
            dma((2, NC)),
            dma((7, NC)),
            dma((4, NC)),
            dma((NC,)),
            dma((2, NC)),
            dma((3, NC)),
            dma((7, NC)),
            dma((3, NC)),
            dma((4, NC)),
            dma((3,)), dma((4,)),
            dma((3,)), dma((4,)),
            dma((3,)), dma((3,)),
            dma((3,)), dma((4,)),
            dma((3, 4)), dma((4, 4)),
        ],
        compiler_params=pltpu.CompilerParams(
            collective_id=0, has_side_effects=True, vmem_limit_bytes=60 * 1024 * 1024
        ),
    )(queries, passages, rt, st, mc, mx, weights[:, None])
    return loss.reshape(rows), gq, gp


def solution(mesh):
    in_specs = (
        P(("grp", "blk"), None),
        P(("grp", "blk"), None),
        P(("grp", "blk"), None),
        P(("grp", "blk")),
    )
    out_specs = (P(("grp", "blk")), P(("grp", "blk"), None), P(("grp", "blk"), None))
    chunks = 8
    return jax.shard_map(
        functools.partial(per_device, chunks, mesh.shape["blk"] // 4),
        mesh=mesh, in_specs=in_specs, out_specs=out_specs, check_vma=False,
    )
```

```python
import functools

import jax
import jax.numpy as jnp
from jax import lax
from jax.experimental import pallas as pl
from jax.experimental.pallas import tpu as pltpu
from jax.sharding import PartitionSpec as P

MESH = pl.DeviceIdType.MESH
TEMP = 50.0
SLOTS = 32
LAG = 4
NEG = -3.0e38
F32, BF16 = jnp.float32, jnp.bfloat16


def nt(a, b):
    return lax.dot_general(a, b, (((1,), (1,)), ((), ())), preferred_element_type=F32)


def tn(a, b):
    return lax.dot_general(a, b, (((0,), (0,)), ((), ())), preferred_element_type=F32)


def nn(a, b):
    return lax.dot_general(a, b, (((1,), (0,)), ((), ())), preferred_element_type=F32)


def kernel(
    NC, Y, CAP, q_hbm, p_hbm, hidx, wrow, loss, gq_hbm, gp_hbm,
    col, bw, tr, xs, xr, ob, rt, st, rx, sc, rxo, pk, mx, wm, acc, wts, mts, wtw, mtx, oq, op,
    ld_s, st_s, z_s, col_r, tr_r, own_s, win_s, bw_r, x_s, x_r,
    rx_s, rx_r, sc_s, sc_r, ro_s, ro_r, ww_s, ww_r, mt_s, mt_r,
):
    rows = 128
    dc = gq_hbm.shape[1] // NC
    packed = 4 * CAP
    g = lax.axis_index("grp")
    b = lax.axis_index("blk")
    p, x = g // 4, g % 4
    y, h, c = b // 4, (b // 2) % 2, b % 2
    z = h * 4 + p
    loop = 4 * Y
    m = p // 2
    outer = (p == 0) | (p == 3)
    inner = jnp.logical_not(outer)

    def a(k):
        return k + m * (3 - 2 * k)

    def zdev(zz):
        zz = (zz + 8) % 8
        return ((zz % 4) * 4 + x, y * 4 + (zz // 4) * 2 + c)

    def ydev(yy, cc):
        return (g, ((yy + Y) % Y) * 4 + h * 2 + cc)

    def bdev(off):
        return (g, (b + off + loop) % loop)

    def xdev(xx, pp):
        return (pp * 4 + xx, b)

    z_in, z_out = zdev(z + 1 - 2 * m), zdev(z - 1 + 2 * m)

    def rcopy(src, dst, ssem, rsem, dev):
        return pltpu.make_async_remote_copy(
            src_ref=src, dst_ref=dst, send_sem=ssem, recv_sem=rsem, device_id=dev, device_id_type=MESH
        )

    def got(ref, rsem):
        rcopy(ref, ref, rsem, rsem, bdev(1)).wait_recv()

    def sent(ref, ssem):
        rcopy(ref, ref, ssem, ssem, bdev(1)).wait_send()

    barrier = pltpu.get_barrier_semaphore()

    def hello(dev):
        pl.semaphore_signal(barrier, inc=1, device_id=dev, device_id_type=MESH)

    for k in range(1, 16):
        hello(((g + k) % 16, b))
    for off in (1, 2, 3, 4):
        hello(bdev(off))
        hello(bdev(-off))
    hello(bdev(5 - 10 * c))

    @pl.when(outer)
    def _():
        hello(z_out)

    def load(src, i, cc):
        return pltpu.make_async_copy(
            src.at[:, pl.ds(pl.multiple_of(cc * dc, dc), dc)], col.at[p, cc, i], ld_s.at[i, cc]
        )

    def start_load(cc, carry):
        load(p_hbm, 0, cc).start()
        load(q_hbm, 1, cc).start()
        return carry

    lax.fori_loop(0, NC, start_load, 0)

    ri = lax.broadcasted_iota(jnp.int32, (rows, rows), 0)
    ci = lax.broadcasted_iota(jnp.int32, (rows, rows), 1)
    target = lax.div(hidx[...], jnp.full((3, rows), loop * rows, jnp.int32))
    wanted = lax.rem(hidx[...], jnp.full((3, rows), rows, jnp.int32)).astype(F32)
    gi = lax.broadcasted_iota(jnp.int32, (16, rows), 0)
    named = jnp.zeros((16, rows), F32)
    row = jnp.zeros((16, rows), F32)
    for k in range(3):
        hit = gi == target[k : k + 1]
        named += jnp.where(hit, 1.0, 0.0)
        row += jnp.where(hit, wanted[k : k + 1], 0.0)
    rank = nn(named.astype(BF16), jnp.where(ri < ci, 1.0, 0.0).astype(BF16))
    rank = jnp.where(named > 0.5, rank, -1.0).astype(jnp.int32)
    slot = lax.broadcasted_iota(jnp.int32, (SLOTS, rows), 0)
    lane = lax.broadcasted_iota(jnp.int32, (SLOTS, rows), 1).astype(F32)
    for k in range(16):
        pick = slot == rank[k : k + 1]
        st[k // 4, k % 4] = jnp.where(pick, 1.0, 0.0).astype(BF16)
        slot_row = jnp.max(jnp.where(pick, row[k : k + 1], -1.0), axis=1, keepdims=True)
        rt[k // 4, k % 4] = jnp.where(slot_row == lane, 1.0, 0.0).astype(BF16)

    @pl.when(outer)
    def _():
        def clear(cc, carry):
            col[a(1), cc, :, packed:, :] = jnp.zeros((2, rows - packed, dc), BF16)
            return carry

        lax.fori_loop(0, NC, clear, 0)

    pl.semaphore_wait(barrier, 25 - ((p + 1) // 2) % 2)

    def own(cc):
        load(p_hbm, 0, cc).wait()
        load(q_hbm, 1, cc).wait()
        rcopy(col.at[p, cc], col.at[p, cc], z_s.at[0, cc], col_r.at[p, cc], z_in).start()
        pdst = 2 - 2 * c
        rcopy(col.at[p, cc, 0], bw.at[pdst, cc], own_s.at[0, cc], bw_r.at[pdst, cc], ydev(y - 1 + c, 1 - c)).start()
        qdst = 3 + 2 * c
        rcopy(col.at[p, cc, 1], bw.at[qdst, cc], own_s.at[1, cc], bw_r.at[qdst, cc], ydev(y + c, 1 - c)).start()

    def own_out(cc):
        @pl.when(inner)
        def _():
            for i in range(2):
                ob[cc, i] = nn(pk[i], col[p, cc, i]).astype(BF16)
            rcopy(
                ob.at[cc, :, pl.ds(0, packed)], col.at[p, cc, :, pl.ds(0, packed)],
                z_s.at[1, cc], col_r.at[p, cc], z_out,
            ).start()

    own(0)
    own(1)

    @pl.when(outer)
    def _():
        for k in range(4):
            rcopy(rt.at[a(1), k], rxo.at[x], ro_s.at[k], ro_r.at[x], xdev(k, a(1))).start()

    for dx in (1, 2, 3):
        xd = (x + dx) % 4
        rcopy(rt.at[:, xd], rx.at[:, x], rx_s.at[dx - 1], rx_r.at[x], xdev(xd, p)).start()
        pd = (p + dx) % 4
        rcopy(st.at[pd], sc.at[p], sc_s.at[dx - 1], sc_r.at[p], xdev(x, pd)).start()
    rx[:, x] = rt[:, x]
    sc[p] = st[p]
    mtx[x, p] = jnp.zeros((SLOTS, rows), BF16)
    acc[...] = jnp.zeros_like(acc)
    wm[...] = jnp.broadcast_to(wrow[...], (rows, rows)).T
    for k in range(4):
        mx[k] = st[:, (x + k) % 4].reshape(rows, rows).astype(F32).T

    unpack = jnp.where((ri % SLOTS < CAP) & (ci == (ri // SLOTS) * CAP + ri % SLOTS), 1.0, 0.0).astype(BF16)

    @pl.when(inner)
    def _():
        for k in range(4):
            got(rxo.at[k], ro_r.at[k])
        pk[0] = tn(unpack, rxo[...].reshape(rows, rows)).astype(BF16)
        pk[1] = tn(unpack, st[a(0)].reshape(rows, rows)).astype(BF16)

    own_out(0)
    own_out(1)
    for dx in (1, 2, 3):
        got(rx.at[:, (x + dx) % 4], rx_r.at[(x + dx) % 4])
        got(sc.at[(p + dx) % 4], sc_r.at[(p + dx) % 4])

    @pl.when(outer)
    def _():
        rx[a(1)] = unpack.reshape(4, SLOTS, rows)
        sc[a(1)] = unpack.reshape(4, SLOTS, rows)

    def fwd_col(l, cc, k, dev):
        got(col.at[l, cc], col_r.at[l, cc])
        rcopy(col.at[l, cc], col.at[l, cc], z_s.at[k, cc], col_r.at[l, cc], dev).start()

    def to_win(src, cc, k, dev, hh):
        pi, qi = 1 + 5 * hh, 6 - 2 * hh
        rcopy(src.at[0], bw.at[pi, cc], z_s.at[k, cc], bw_r.at[pi, cc], dev).start()
        rcopy(src.at[1], bw.at[qi, cc], z_s.at[k + 1, cc], bw_r.at[qi, cc], dev).start()

    def hop12(cc):
        @pl.when(outer)
        def _():
            got(col.at[a(2), cc], col_r.at[a(2), cc])
            rcopy(col.at[a(2), cc], tr.at[cc], z_s.at[2, cc], tr_r.at[cc], z_out).start()

        @pl.when(inner)
        def _():
            fwd_col(a(0), cc, 2, z_in)
            fwd_col(a(2), cc, 3, z_out)
            fwd_col(a(3), cc, 4, z_out)

    def hop3(cc):
        @pl.when(outer)
        def _():
            got(col.at[a(3), cc], col_r.at[a(3), cc])
            to_win(col.at[a(3), cc], cc, 3, z_out, 1 - h)
            got(tr.at[cc], tr_r.at[cc])
            to_win(tr.at[cc], cc, 5, z_in, h)
            part = col.at[a(1), cc, :, pl.ds(0, packed)]
            got(part, col_r.at[a(1), cc])

    def win(cc):
        wi = 1 + 3 * h
        got(bw.at[wi, cc], bw_r.at[wi, cc])
        d = h * (5 - 2 * c) + (1 - h) * 2 * c
        rcopy(bw.at[wi, cc], bw.at[d, cc], win_s.at[0, cc], bw_r.at[d, cc], ydev(y, 1 - c)).start()
        got(bw.at[6, cc], bw_r.at[6, cc])
        for c2 in (0, 1):
            d = h * (1 - c2 + c) + (1 - h) * (4 + c2 - c)
            rcopy(
                bw.at[6, cc], bw.at[d, cc], win_s.at[1 + c2, cc], bw_r.at[d, cc], ydev(y + 1 - 2 * h, c2)
            ).start()

    def pick_rows(cc):
        for l in range(4):
            rows_p = nn(rx[l].reshape(4 * SLOTS, rows), col[l, cc, 0]).astype(BF16)
            xs[:, cc, 0, l * SLOTS : (l + 1) * SLOTS, :] = rows_p.reshape(4, SLOTS, dc)
            rows_q = nn(sc[l].reshape(4 * SLOTS, rows), col[l, cc, 1]).astype(BF16)
            xs[:, cc, 1, l * SLOTS : (l + 1) * SLOTS, :] = rows_q.reshape(4, SLOTS, dc)
        for dx in (2, 1, 3):
            xd = (x + dx) % 4
            rcopy(xs.at[xd, cc], xr.at[x, cc], x_s.at[dx - 1, cc], x_r.at[x, cc], xdev(xd, p)).start()

    def score(cc):
        for i in (0, 2, 3, 5):
            got(bw.at[i, cc], bw_r.at[i, cc])
        got(bw.at[4 - 3 * h, cc], bw_r.at[4 - 3 * h, cc])
        for dx in (1, 2, 3):
            got(xr.at[(x + dx) % 4, cc], x_r.at[(x + dx) % 4, cc])
        q = col[p, cc, 1]
        acc[0] += nt(q, col[p, cc, 0])
        acc[4] += nt(q, xs[x, cc, 0])
        for s in range(3):
            acc[1 + s] += nt(q, bw[s, cc])
            acc[5 + s] += nt(q, xr[(x + 1 + s) % 4, cc, 0])

    def step(t, carry):
        @pl.when(t + 2 < NC)
        def _():
            own(t + 2)
            own_out(t + 2)

        @pl.when(t < NC)
        def _():
            hop12(t)

        @pl.when((t >= 1) & (t < NC + 1))
        def _():
            hop3(t - 1)

        @pl.when((t >= 2) & (t < NC + 2))
        def _():
            win(t - 2)

        @pl.when((t >= 1) & (t < NC + 1))
        def _():
            pick_rows(t - 1)

        @pl.when(t >= LAG)
        def _():
            score(t - LAG)

        return carry

    lax.fori_loop(0, NC + LAG, step, 0)

    w = wm[...]
    scores = [TEMP * acc[k] for k in range(4)]
    scores += [jnp.where(mx[k] > 0.5, TEMP * acc[4 + k], NEG) for k in range(4)]
    top = scores[0]
    for k in range(1, 8):
        top = jnp.maximum(top, scores[k])
    top = jnp.max(top, axis=1, keepdims=True)
    total = jnp.zeros((rows, rows), F32)
    for k in range(8):
        e = jnp.exp(scores[k] - top)
        total += e if k < 4 else jnp.where(mx[k - 4] > 0.5, e, 0.0)
    log_total = top + jnp.log(jnp.sum(total, axis=1, keepdims=True))
    for k in range(8):
        e = w * jnp.exp(scores[k] - log_total)
        wts[k] = (e if k < 4 else jnp.where(mx[k - 4] > 0.5, e, 0.0)).astype(BF16)
    ones = jnp.ones((rows, rows), BF16)
    for k in range(4):
        by_slot = tn(wts[4 + k], ones)
        want = rt[:, (x + k) % 4].reshape(rows, rows).astype(F32)
        mts[k] = (by_slot * want).astype(BF16).reshape(4, SLOTS, rows)

    for s in range(3):
        rcopy(wts.at[1 + s], wtw.at[s], ww_s.at[s], ww_r.at[s], bdev(1 + s)).start()
        pd = (p + 1 + s) % 4
        rcopy(mts.at[0, pd], mtx.at[x, p], mt_s.at[0, pd], mt_r.at[x, p], xdev(x, pd)).start()
        xd = (x + 1 + s) % 4
        for l in range(4):
            rcopy(mts.at[1 + s, l], mtx.at[x, p], mt_s.at[1 + s, l], mt_r.at[x, p], xdev(xd, l)).start()

    loss[...] = jnp.sum(jnp.where(ri == ci, log_total - scores[0], 0.0), axis=0, keepdims=True)

    def store(src, dst, i, cc):
        return pltpu.make_async_copy(
            src.at[cc], dst.at[:, pl.ds(pl.multiple_of(cc * dc, dc), dc)], st_s.at[i, cc]
        )

    def queries(cc, carry):
        own_p = col[p, cc, 0]
        tot = nn(wts[0], own_p)
        tot += nn(wts[4], xs[x, cc, 0])
        for s in range(3):
            tot += nn(wts[1 + s], bw[s, cc])
            tot += nn(wts[5 + s], xr[(x + 1 + s) % 4, cc, 0])
        oq[cc] = (TEMP * (tot - wm[:, :1] * own_p.astype(F32))).astype(BF16)
        store(oq, gq_hbm, 0, cc).start()
        return carry

    lax.fori_loop(0, NC, queries, 0)

    for s in range(3):
        got(wtw.at[s], ww_r.at[s])
        pd, xd = (p + 1 + s) % 4, (x + 1 + s) % 4
        got(mtx.at[x, pd], mt_r.at[x, pd])
        for l in range(4):
            got(mtx.at[xd, l], mt_r.at[xd, l])

    def passages(cc, carry):
        own_q = col[p, cc, 1]
        tot = tn(wts[0], own_q)
        tot += tn(mtx[x].reshape(rows, rows), xs[x, cc, 1])
        for s in range(3):
            xd = (x + 1 + s) % 4
            tot += tn(wtw[s], bw[3 + s, cc])
            tot += tn(mtx[xd].reshape(rows, rows), xr[xd, cc, 1])
        op[cc] = (TEMP * (tot - wm[:, :1] * own_q.astype(F32))).astype(BF16)
        store(op, gp_hbm, 1, cc).start()
        return carry

    lax.fori_loop(0, NC, passages, 0)

    def drain(cc, carry):
        store(oq, gq_hbm, 0, cc).wait()
        store(op, gp_hbm, 1, cc).wait()
        sent(col.at[p, cc], z_s.at[0, cc])
        sent(col.at[p, cc, 0], own_s.at[0, cc])
        sent(col.at[p, cc, 1], own_s.at[1, cc])
        sent(col.at[p, cc], z_s.at[2, cc])
        for k in range(3):
            sent(bw.at[6, cc], win_s.at[k, cc])
            sent(xs.at[0, cc], x_s.at[k, cc])

        @pl.when(outer)
        def _():
            for k in (3, 4, 5, 6):
                sent(col.at[p, cc, 0], z_s.at[k, cc])

        @pl.when(inner)
        def _():
            sent(ob.at[cc, :, pl.ds(0, packed)], z_s.at[1, cc])
            for k in (3, 4):
                sent(col.at[p, cc], z_s.at[k, cc])

        return carry

    lax.fori_loop(0, NC, drain, 0)

    @pl.when(outer)
    def _():
        for k in range(4):
            sent(rt.at[0, 0], ro_s.at[k])

    for s in range(3):
        sent(rt.at[:, 0], rx_s.at[s])
        sent(st.at[0], sc_s.at[s])
        sent(wts.at[1 + s], ww_s.at[s])
        sent(mts.at[0, 0], mt_s.at[0, (p + 1 + s) % 4])
        for l in range(4):
            sent(mts.at[1 + s, l], mt_s.at[1 + s, l])


def per_device(NC, Y, queries, passages, hard_index, weights):
    rows, width = queries.shape
    cap = max(2, (3 * rows + 14) // 15)
    dc = width // NC
    dma = pltpu.SemaphoreType.DMA
    vmem = pl.BlockSpec(memory_space=pltpu.VMEM)
    hbm = pl.BlockSpec(memory_space=pl.ANY)
    loss, gq, gp = pl.pallas_call(
        functools.partial(kernel, NC, Y, cap),
        out_shape=(
            jax.ShapeDtypeStruct((1, rows), F32),
            jax.ShapeDtypeStruct((rows, width), BF16),
            jax.ShapeDtypeStruct((rows, width), BF16),
        ),
        in_specs=[hbm, hbm, vmem, vmem],
        out_specs=(vmem, hbm, hbm),
        scratch_shapes=[
            pltpu.VMEM((4, NC, 2, rows, dc), BF16),
            pltpu.VMEM((7, NC, rows, dc), BF16),
            pltpu.VMEM((NC, 2, rows, dc), BF16),
            pltpu.VMEM((4, NC, 2, rows, dc), BF16),
            pltpu.VMEM((4, NC, 2, rows, dc), BF16),
            pltpu.VMEM((NC, 2, rows, dc), BF16),
            pltpu.VMEM((4, 4, SLOTS, rows), BF16),
            pltpu.VMEM((4, 4, SLOTS, rows), BF16),
            pltpu.VMEM((4, 4, SLOTS, rows), BF16),
            pltpu.VMEM((4, 4, SLOTS, rows), BF16),
            pltpu.VMEM((4, SLOTS, rows), BF16),
            pltpu.VMEM((2, rows, rows), BF16),
            pltpu.VMEM((4, rows, rows), F32),
            pltpu.VMEM((rows, rows), F32),
            pltpu.VMEM((8, rows, rows), F32),
            pltpu.VMEM((8, rows, rows), BF16),
            pltpu.VMEM((4, 4, SLOTS, rows), BF16),
            pltpu.VMEM((3, rows, rows), BF16),
            pltpu.VMEM((4, 4, SLOTS, rows), BF16),
            pltpu.VMEM((NC, rows, dc), BF16),
            pltpu.VMEM((NC, rows, dc), BF16),
            dma((2, NC)),
            dma((2, NC)),
            dma((7, NC)),
            dma((4, NC)),
            dma((NC,)),
            dma((2, NC)),
            dma((3, NC)),
            dma((7, NC)),
            dma((3, NC)),
            dma((4, NC)),
            dma((3,)), dma((4,)),
            dma((3,)), dma((4,)),
            dma((4,)), dma((4,)),
            dma((3,)), dma((3,)),
            dma((4, 4)), dma((4, 4)),
        ],
        compiler_params=pltpu.CompilerParams(
            collective_id=0, has_side_effects=True, vmem_limit_bytes=60 * 1024 * 1024
        ),
    )(queries, passages, hard_index.T, weights.reshape(1, rows))
    return loss.reshape(rows), gq, gp


def solution(mesh):
    in_specs = (
        P(("grp", "blk"), None),
        P(("grp", "blk"), None),
        P(("grp", "blk"), None),
        P(("grp", "blk")),
    )
    out_specs = (P(("grp", "blk")), P(("grp", "blk"), None), P(("grp", "blk"), None))
    chunks = 16
    return jax.shard_map(
        functools.partial(per_device, chunks, mesh.shape["blk"] // 4),
        mesh=mesh, in_specs=in_specs, out_specs=out_specs, check_vma=False,
    )
```

```python
import functools

import jax
import jax.numpy as jnp
from jax import lax
from jax.experimental import pallas as pl
from jax.experimental.pallas import tpu as pltpu
from jax.sharding import PartitionSpec as P

MESH = pl.DeviceIdType.MESH
TEMP = 50.0
SLOTS = 32
AHEAD = 1
LAG_HOP2, LAG_HOP3, LAG_OUT, LAG_WIN, LAG_PICK, LAG_SCORE = 1, 1, 1, 2, 1, 4
NEG = -3.0e38
F32, BF16 = jnp.float32, jnp.bfloat16


def nt(a, b):
    return lax.dot_general(a, b, (((1,), (1,)), ((), ())), preferred_element_type=F32)


def tn(a, b):
    return lax.dot_general(a, b, (((0,), (0,)), ((), ())), preferred_element_type=F32)


def nn(a, b):
    return lax.dot_general(a, b, (((1,), (0,)), ((), ())), preferred_element_type=F32)


def kernel(
    NC, Y, CAP, q_hbm, p_hbm, hidx, wrow, loss, gq_hbm, gp_hbm,
    col, bw, tr, xs, xr, ob, rt, st, rx, sc, rxo, pk, mx, wm, acc, wts, mts, wtw, mtx, oq, op,
    ld_s, st_s, z_s, col_r, tr_r, own_s, win_s, bw_r, x_s, x_r,
    rx_s, rx_r, sc_s, sc_r, ro_s, ro_r, ww_s, ww_r, mt_s, mt_r,
):
    rows = 128
    dc = gq_hbm.shape[1] // NC
    packed = 4 * CAP
    g = lax.axis_index("grp")
    b = lax.axis_index("blk")
    p, x = g // 4, g % 4
    y, h, c = b // 4, (b // 2) % 2, b % 2
    z = h * 4 + p
    loop = 4 * Y
    m = p // 2
    outer = (p == 0) | (p == 3)
    inner = jnp.logical_not(outer)

    def a(k):
        return k + m * (3 - 2 * k)

    def zdev(zz):
        zz = (zz + 8) % 8
        return ((zz % 4) * 4 + x, y * 4 + (zz // 4) * 2 + c)

    def ydev(yy, cc):
        return (g, ((yy + Y) % Y) * 4 + h * 2 + cc)

    def bdev(off):
        return (g, (b + off + loop) % loop)

    def xdev(xx, pp):
        return (pp * 4 + xx, b)

    z_in, z_out = zdev(z + 1 - 2 * m), zdev(z - 1 + 2 * m)

    def rcopy(src, dst, ssem, rsem, dev):
        return pltpu.make_async_remote_copy(
            src_ref=src, dst_ref=dst, send_sem=ssem, recv_sem=rsem, device_id=dev, device_id_type=MESH
        )

    def got(ref, rsem):
        rcopy(ref, ref, rsem, rsem, bdev(1)).wait_recv()

    def sent(ref, ssem):
        rcopy(ref, ref, ssem, ssem, bdev(1)).wait_send()

    barrier = pltpu.get_barrier_semaphore()

    def hello(dev):
        pl.semaphore_signal(barrier, inc=1, device_id=dev, device_id_type=MESH)

    for k in range(1, 16):
        hello(((g + k) % 16, b))
    for off in (1, 2, 3, 4):
        hello(bdev(off))
        hello(bdev(-off))
    hello(bdev(5 - 10 * c))

    @pl.when(outer)
    def _():
        hello(z_out)

    def load(src, i, cc):
        return pltpu.make_async_copy(
            src.at[:, pl.ds(pl.multiple_of(cc * dc, dc), dc)], col.at[p, cc, i], ld_s.at[i, cc]
        )

    def start_load(cc, carry):
        load(p_hbm, 0, cc).start()
        load(q_hbm, 1, cc).start()
        return carry

    lax.fori_loop(0, NC, start_load, 0)

    ri = lax.broadcasted_iota(jnp.int32, (rows, rows), 0)
    ci = lax.broadcasted_iota(jnp.int32, (rows, rows), 1)
    target = lax.div(hidx[...], jnp.full((3, rows), loop * rows, jnp.int32))
    wanted = lax.rem(hidx[...], jnp.full((3, rows), rows, jnp.int32)).astype(F32)
    gi = lax.broadcasted_iota(jnp.int32, (16, rows), 0)
    named = jnp.zeros((16, rows), F32)
    row = jnp.zeros((16, rows), F32)
    for k in range(3):
        hit = gi == target[k : k + 1]
        named += jnp.where(hit, 1.0, 0.0)
        row += jnp.where(hit, wanted[k : k + 1], 0.0)
    rank = nn(named.astype(BF16), jnp.where(ri < ci, 1.0, 0.0).astype(BF16))
    rank = jnp.where(named > 0.5, rank, -1.0).astype(jnp.int32)
    slot = lax.broadcasted_iota(jnp.int32, (SLOTS, rows), 0)
    lane = lax.broadcasted_iota(jnp.int32, (SLOTS, rows), 1).astype(F32)
    for k in range(16):
        pick = slot == rank[k : k + 1]
        st[k // 4, k % 4] = jnp.where(pick, 1.0, 0.0).astype(BF16)
        slot_row = jnp.max(jnp.where(pick, row[k : k + 1], -1.0), axis=1, keepdims=True)
        rt[k // 4, k % 4] = jnp.where(slot_row == lane, 1.0, 0.0).astype(BF16)

    @pl.when(outer)
    def _():
        def clear(cc, carry):
            col[a(1), cc, :, packed:, :] = jnp.zeros((2, rows - packed, dc), BF16)
            return carry

        lax.fori_loop(0, NC, clear, 0)

    pl.semaphore_wait(barrier, 25 - ((p + 1) // 2) % 2)

    def own(cc):
        load(p_hbm, 0, cc).wait()
        load(q_hbm, 1, cc).wait()
        rcopy(col.at[p, cc], col.at[p, cc], z_s.at[0, cc], col_r.at[p, cc], z_in).start()
        pdst = 2 - 2 * c
        rcopy(col.at[p, cc, 0], bw.at[pdst, cc], own_s.at[0, cc], bw_r.at[pdst, cc], ydev(y - 1 + c, 1 - c)).start()
        qdst = 3 + 2 * c
        rcopy(col.at[p, cc, 1], bw.at[qdst, cc], own_s.at[1, cc], bw_r.at[qdst, cc], ydev(y + c, 1 - c)).start()

    def own_out(cc):
        @pl.when(inner)
        def _():
            for i in range(2):
                ob[cc, i] = nn(pk[i], col[p, cc, i]).astype(BF16)
            rcopy(
                ob.at[cc, :, pl.ds(0, packed)], col.at[p, cc, :, pl.ds(0, packed)],
                z_s.at[1, cc], col_r.at[p, cc], z_out,
            ).start()

    for k in range(AHEAD):
        own(k)

    @pl.when(outer)
    def _():
        for k in range(4):
            rcopy(rt.at[a(1), k], rxo.at[x], ro_s.at[k], ro_r.at[x], xdev(k, a(1))).start()

    for dx in (1, 2, 3):
        xd = (x + dx) % 4
        rcopy(rt.at[:, xd], rx.at[:, x], rx_s.at[dx - 1], rx_r.at[x], xdev(xd, p)).start()
        pd = (p + dx) % 4
        rcopy(st.at[pd], sc.at[p], sc_s.at[dx - 1], sc_r.at[p], xdev(x, pd)).start()
    rx[:, x] = rt[:, x]
    sc[p] = st[p]
    mtx[x, p] = jnp.zeros((SLOTS, rows), BF16)
    acc[...] = jnp.zeros_like(acc)
    wm[...] = jnp.broadcast_to(wrow[...], (rows, rows)).T
    for k in range(4):
        mx[k] = st[:, (x + k) % 4].reshape(rows, rows).astype(F32).T

    unpack = jnp.where((ri % SLOTS < CAP) & (ci == (ri // SLOTS) * CAP + ri % SLOTS), 1.0, 0.0).astype(BF16)

    @pl.when(inner)
    def _():
        for k in range(4):
            got(rxo.at[k], ro_r.at[k])
        pk[0] = tn(unpack, rxo[...].reshape(rows, rows)).astype(BF16)
        pk[1] = tn(unpack, st[a(0)].reshape(rows, rows)).astype(BF16)

    for dx in (1, 2, 3):
        got(rx.at[:, (x + dx) % 4], rx_r.at[(x + dx) % 4])
        got(sc.at[(p + dx) % 4], sc_r.at[(p + dx) % 4])

    @pl.when(outer)
    def _():
        rx[a(1)] = unpack.reshape(4, SLOTS, rows)
        sc[a(1)] = unpack.reshape(4, SLOTS, rows)

    def fwd_col(l, cc, k, dev):
        got(col.at[l, cc], col_r.at[l, cc])
        rcopy(col.at[l, cc], col.at[l, cc], z_s.at[k, cc], col_r.at[l, cc], dev).start()

    def to_win(src, cc, k, dev, hh):
        pi, qi = 1 + 5 * hh, 6 - 2 * hh
        rcopy(src.at[0], bw.at[pi, cc], z_s.at[k, cc], bw_r.at[pi, cc], dev).start()
        rcopy(src.at[1], bw.at[qi, cc], z_s.at[k + 1, cc], bw_r.at[qi, cc], dev).start()

    def hop1(cc):
        @pl.when(outer)
        def _():
            got(col.at[a(2), cc], col_r.at[a(2), cc])
            rcopy(col.at[a(2), cc], tr.at[cc], z_s.at[2, cc], tr_r.at[cc], z_out).start()

        @pl.when(inner)
        def _():
            fwd_col(a(0), cc, 2, z_in)
            fwd_col(a(2), cc, 3, z_out)

    def hop2(cc):
        @pl.when(inner)
        def _():
            fwd_col(a(3), cc, 4, z_out)

    def hop3(cc):
        @pl.when(outer)
        def _():
            got(col.at[a(3), cc], col_r.at[a(3), cc])
            to_win(col.at[a(3), cc], cc, 3, z_out, 1 - h)
            got(tr.at[cc], tr_r.at[cc])
            to_win(tr.at[cc], cc, 5, z_in, h)

    def win(cc):
        wi = 1 + 3 * h
        got(bw.at[wi, cc], bw_r.at[wi, cc])
        d = h * (5 - 2 * c) + (1 - h) * 2 * c
        rcopy(bw.at[wi, cc], bw.at[d, cc], win_s.at[0, cc], bw_r.at[d, cc], ydev(y, 1 - c)).start()
        got(bw.at[6, cc], bw_r.at[6, cc])
        for c2 in (0, 1):
            d = h * (1 - c2 + c) + (1 - h) * (4 + c2 - c)
            rcopy(
                bw.at[6, cc], bw.at[d, cc], win_s.at[1 + c2, cc], bw_r.at[d, cc], ydev(y + 1 - 2 * h, c2)
            ).start()

    def pick_rows(cc):
        @pl.when(outer)
        def _():
            got(col.at[a(1), cc, :, pl.ds(0, packed)], col_r.at[a(1), cc])

        for l in range(4):
            rows_p = nn(rx[l].reshape(4 * SLOTS, rows), col[l, cc, 0]).astype(BF16)
            xs[:, cc, 0, l * SLOTS : (l + 1) * SLOTS, :] = rows_p.reshape(4, SLOTS, dc)
            rows_q = nn(sc[l].reshape(4 * SLOTS, rows), col[l, cc, 1]).astype(BF16)
            xs[:, cc, 1, l * SLOTS : (l + 1) * SLOTS, :] = rows_q.reshape(4, SLOTS, dc)
        for dx in (2, 1, 3):
            xd = (x + dx) % 4
            rcopy(xs.at[xd, cc], xr.at[x, cc], x_s.at[dx - 1, cc], x_r.at[x, cc], xdev(xd, p)).start()

    def score(cc):
        for i in (0, 2, 3, 5):
            got(bw.at[i, cc], bw_r.at[i, cc])
        got(bw.at[4 - 3 * h, cc], bw_r.at[4 - 3 * h, cc])
        for dx in (1, 2, 3):
            got(xr.at[(x + dx) % 4, cc], x_r.at[(x + dx) % 4, cc])
        q = col[p, cc, 1]
        acc[0] += nt(q, col[p, cc, 0])
        acc[4] += nt(q, xs[x, cc, 0])
        for s in range(3):
            acc[1 + s] += nt(q, bw[s, cc])
            acc[5 + s] += nt(q, xr[(x + 1 + s) % 4, cc, 0])

    def step(t, carry):
        def stage(lag, part):
            @pl.when((t >= lag) & (t < NC + lag))
            def _():
                part(t - lag)

        @pl.when(t + AHEAD < NC)
        def _():
            own(t + AHEAD)

        stage(0, hop1)
        stage(LAG_HOP2, hop2)
        stage(LAG_HOP3, hop3)
        stage(LAG_OUT, own_out)
        stage(LAG_WIN, win)
        stage(LAG_PICK, pick_rows)
        stage(LAG_SCORE, score)
        return carry

    lax.fori_loop(0, NC + LAG_SCORE, step, 0)

    w = wm[...]
    scores = [TEMP * acc[k] for k in range(4)]
    scores += [jnp.where(mx[k] > 0.5, TEMP * acc[4 + k], NEG) for k in range(4)]
    top = scores[0]
    for k in range(1, 8):
        top = jnp.maximum(top, scores[k])
    top = jnp.max(top, axis=1, keepdims=True)
    total = jnp.zeros((rows, rows), F32)
    for k in range(8):
        e = jnp.exp(scores[k] - top)
        total += e if k < 4 else jnp.where(mx[k - 4] > 0.5, e, 0.0)
    log_total = top + jnp.log(jnp.sum(total, axis=1, keepdims=True))
    for k in range(8):
        e = w * jnp.exp(scores[k] - log_total)
        wts[k] = (e if k < 4 else jnp.where(mx[k - 4] > 0.5, e, 0.0)).astype(BF16)
    ones = jnp.ones((rows, rows), BF16)
    for k in range(4):
        by_slot = tn(wts[4 + k], ones)
        want = rt[:, (x + k) % 4].reshape(rows, rows).astype(F32)
        mts[k] = (by_slot * want).astype(BF16).reshape(4, SLOTS, rows)

    for s in range(3):
        rcopy(wts.at[1 + s], wtw.at[s], ww_s.at[s], ww_r.at[s], bdev(1 + s)).start()
        pd = (p + 1 + s) % 4
        rcopy(mts.at[0, pd], mtx.at[x, p], mt_s.at[0, pd], mt_r.at[x, p], xdev(x, pd)).start()
        xd = (x + 1 + s) % 4
        for l in range(4):
            rcopy(mts.at[1 + s, l], mtx.at[x, p], mt_s.at[1 + s, l], mt_r.at[x, p], xdev(xd, l)).start()

    loss[...] = jnp.sum(jnp.where(ri == ci, log_total - scores[0], 0.0), axis=0, keepdims=True)

    def store(src, dst, i, cc):
        return pltpu.make_async_copy(
            src.at[cc], dst.at[:, pl.ds(pl.multiple_of(cc * dc, dc), dc)], st_s.at[i, cc]
        )

    def queries(cc, carry):
        own_p = col[p, cc, 0]
        tot = nn(wts[0], own_p)
        tot += nn(wts[4], xs[x, cc, 0])
        for s in range(3):
            tot += nn(wts[1 + s], bw[s, cc])
            tot += nn(wts[5 + s], xr[(x + 1 + s) % 4, cc, 0])
        oq[cc] = (TEMP * (tot - wm[:, :1] * own_p.astype(F32))).astype(BF16)
        store(oq, gq_hbm, 0, cc).start()
        return carry

    lax.fori_loop(0, NC, queries, 0)

    for s in range(3):
        got(wtw.at[s], ww_r.at[s])
        pd, xd = (p + 1 + s) % 4, (x + 1 + s) % 4
        got(mtx.at[x, pd], mt_r.at[x, pd])
        for l in range(4):
            got(mtx.at[xd, l], mt_r.at[xd, l])

    def passages(cc, carry):
        own_q = col[p, cc, 1]
        tot = tn(wts[0], own_q)
        tot += tn(mtx[x].reshape(rows, rows), xs[x, cc, 1])
        for s in range(3):
            xd = (x + 1 + s) % 4
            tot += tn(wtw[s], bw[3 + s, cc])
            tot += tn(mtx[xd].reshape(rows, rows), xr[xd, cc, 1])
        op[cc] = (TEMP * (tot - wm[:, :1] * own_q.astype(F32))).astype(BF16)
        store(op, gp_hbm, 1, cc).start()
        return carry

    lax.fori_loop(0, NC, passages, 0)

    def drain(cc, carry):
        store(oq, gq_hbm, 0, cc).wait()
        store(op, gp_hbm, 1, cc).wait()
        sent(col.at[p, cc], z_s.at[0, cc])
        sent(col.at[p, cc, 0], own_s.at[0, cc])
        sent(col.at[p, cc, 1], own_s.at[1, cc])
        sent(col.at[p, cc], z_s.at[2, cc])
        for k in range(3):
            sent(bw.at[6, cc], win_s.at[k, cc])
            sent(xs.at[0, cc], x_s.at[k, cc])

        @pl.when(outer)
        def _():
            for k in (3, 4, 5, 6):
                sent(col.at[p, cc, 0], z_s.at[k, cc])

        @pl.when(inner)
        def _():
            sent(ob.at[cc, :, pl.ds(0, packed)], z_s.at[1, cc])
            for k in (3, 4):
                sent(col.at[p, cc], z_s.at[k, cc])

        return carry

    lax.fori_loop(0, NC, drain, 0)

    @pl.when(outer)
    def _():
        for k in range(4):
            sent(rt.at[0, 0], ro_s.at[k])

    for s in range(3):
        sent(rt.at[:, 0], rx_s.at[s])
        sent(st.at[0], sc_s.at[s])
        sent(wts.at[1 + s], ww_s.at[s])
        sent(mts.at[0, 0], mt_s.at[0, (p + 1 + s) % 4])
        for l in range(4):
            sent(mts.at[1 + s, l], mt_s.at[1 + s, l])


def per_device(NC, Y, queries, passages, hard_index, weights):
    rows, width = queries.shape
    cap = max(2, (3 * rows + 14) // 15)
    dc = width // NC
    dma = pltpu.SemaphoreType.DMA
    vmem = pl.BlockSpec(memory_space=pltpu.VMEM)
    hbm = pl.BlockSpec(memory_space=pl.ANY)
    loss, gq, gp = pl.pallas_call(
        functools.partial(kernel, NC, Y, cap),
        out_shape=(
            jax.ShapeDtypeStruct((1, rows), F32),
            jax.ShapeDtypeStruct((rows, width), BF16),
            jax.ShapeDtypeStruct((rows, width), BF16),
        ),
        in_specs=[hbm, hbm, vmem, vmem],
        out_specs=(vmem, hbm, hbm),
        scratch_shapes=[
            pltpu.VMEM((4, NC, 2, rows, dc), BF16),
            pltpu.VMEM((7, NC, rows, dc), BF16),
            pltpu.VMEM((NC, 2, rows, dc), BF16),
            pltpu.VMEM((4, NC, 2, rows, dc), BF16),
            pltpu.VMEM((4, NC, 2, rows, dc), BF16),
            pltpu.VMEM((NC, 2, rows, dc), BF16),
            pltpu.VMEM((4, 4, SLOTS, rows), BF16),
            pltpu.VMEM((4, 4, SLOTS, rows), BF16),
            pltpu.VMEM((4, 4, SLOTS, rows), BF16),
            pltpu.VMEM((4, 4, SLOTS, rows), BF16),
            pltpu.VMEM((4, SLOTS, rows), BF16),
            pltpu.VMEM((2, rows, rows), BF16),
            pltpu.VMEM((4, rows, rows), F32),
            pltpu.VMEM((rows, rows), F32),
            pltpu.VMEM((8, rows, rows), F32),
            pltpu.VMEM((8, rows, rows), BF16),
            pltpu.VMEM((4, 4, SLOTS, rows), BF16),
            pltpu.VMEM((3, rows, rows), BF16),
            pltpu.VMEM((4, 4, SLOTS, rows), BF16),
            pltpu.VMEM((NC, rows, dc), BF16),
            pltpu.VMEM((NC, rows, dc), BF16),
            dma((2, NC)),
            dma((2, NC)),
            dma((7, NC)),
            dma((4, NC)),
            dma((NC,)),
            dma((2, NC)),
            dma((3, NC)),
            dma((7, NC)),
            dma((3, NC)),
            dma((4, NC)),
            dma((3,)), dma((4,)),
            dma((3,)), dma((4,)),
            dma((4,)), dma((4,)),
            dma((3,)), dma((3,)),
            dma((4, 4)), dma((4, 4)),
        ],
        compiler_params=pltpu.CompilerParams(
            collective_id=0, has_side_effects=True, vmem_limit_bytes=60 * 1024 * 1024
        ),
    )(queries, passages, hard_index.T, weights.reshape(1, rows))
    return loss.reshape(rows), gq, gp


def solution(mesh):
    in_specs = (
        P(("grp", "blk"), None),
        P(("grp", "blk"), None),
        P(("grp", "blk"), None),
        P(("grp", "blk")),
    )
    out_specs = (P(("grp", "blk")), P(("grp", "blk"), None), P(("grp", "blk"), None))
    chunks = 16
    return jax.shard_map(
        functools.partial(per_device, chunks, mesh.shape["blk"] // 4),
        mesh=mesh, in_specs=in_specs, out_specs=out_specs, check_vma=False,
    )
```

```python
import functools

import jax
import jax.numpy as jnp
from jax import lax
from jax.experimental import pallas as pl
from jax.experimental.pallas import tpu as pltpu
from jax.sharding import PartitionSpec as P

MESH = pl.DeviceIdType.MESH
TEMP = 50.0
SLOTS = 32
AHEAD = 1
LAG_HOP2, LAG_HOP3, LAG_OUT, LAG_WIN, LAG_PICK, LAG_SCORE = 1, 1, 0, 2, 1, 3
NEG = -3.0e38
F32, BF16 = jnp.float32, jnp.bfloat16


def nt(a, b):
    return lax.dot_general(a, b, (((1,), (1,)), ((), ())), preferred_element_type=F32)


def tn(a, b):
    return lax.dot_general(a, b, (((0,), (0,)), ((), ())), preferred_element_type=F32)


def nn(a, b):
    return lax.dot_general(a, b, (((1,), (0,)), ((), ())), preferred_element_type=F32)


def kernel(
    NC, Y, CAP, q_hbm, p_hbm, hidx, wrow, loss, gq_hbm, gp_hbm,
    col, bw, xs, xr, ob, rt, st, rx, sc, rxo, pk, mx, wm, acc, wts, mts, wtw, mtx, oq, op,
    ld_s, st_s, z_s, col_r, own_s, win_s, bw_r, x_s, x_r,
    rx_s, rx_r, sc_s, sc_r, ro_s, ro_r, ww_s, ww_r, mt_s, mt_r,
):
    rows = 128
    dc = gq_hbm.shape[1] // NC
    packed = 4 * CAP
    g = lax.axis_index("grp")
    b = lax.axis_index("blk")
    p, x = g // 4, g % 4
    y, h, c = b // 4, (b // 2) % 2, b % 2
    z = h * 4 + p
    loop = 4 * Y
    m = p // 2
    outer = (p == 0) | (p == 3)
    inner = jnp.logical_not(outer)

    def a(k):
        return k + m * (3 - 2 * k)

    def zdev(zz):
        zz = (zz + 8) % 8
        return ((zz % 4) * 4 + x, y * 4 + (zz // 4) * 2 + c)

    def ydev(yy, cc):
        return (g, ((yy + Y) % Y) * 4 + h * 2 + cc)

    def bdev(off):
        return (g, (b + off + loop) % loop)

    def xdev(xx, pp):
        return (pp * 4 + xx, b)

    z_in, z_out, z_far = zdev(z + 1 - 2 * m), zdev(z - 1 + 2 * m), zdev(z - 2 + 4 * m)

    def rcopy(src, dst, ssem, rsem, dev):
        return pltpu.make_async_remote_copy(
            src_ref=src, dst_ref=dst, send_sem=ssem, recv_sem=rsem, device_id=dev, device_id_type=MESH
        )

    def got(ref, rsem):
        rcopy(ref, ref, rsem, rsem, bdev(1)).wait_recv()

    def sent(ref, ssem):
        rcopy(ref, ref, ssem, ssem, bdev(1)).wait_send()

    barrier = pltpu.get_barrier_semaphore()

    def hello(dev):
        pl.semaphore_signal(barrier, inc=1, device_id=dev, device_id_type=MESH)

    for k in range(1, 16):
        hello(((g + k) % 16, b))
    for off in (1, 2, 3, 4):
        hello(bdev(off))
        hello(bdev(-off))
    hello(bdev(5 - 10 * c))

    hello(z_far)

    @pl.when(outer)
    def _():
        hello(z_out)

    def load(src, i, cc):
        return pltpu.make_async_copy(
            src.at[:, pl.ds(pl.multiple_of(cc * dc, dc), dc)], col.at[p, cc, i], ld_s.at[i, cc]
        )

    def start_load(cc, carry):
        load(p_hbm, 0, cc).start()
        load(q_hbm, 1, cc).start()
        return carry

    lax.fori_loop(0, NC, start_load, 0)

    ri = lax.broadcasted_iota(jnp.int32, (rows, rows), 0)
    ci = lax.broadcasted_iota(jnp.int32, (rows, rows), 1)
    target = lax.div(hidx[...], jnp.full((3, rows), loop * rows, jnp.int32))
    wanted = lax.rem(hidx[...], jnp.full((3, rows), rows, jnp.int32)).astype(F32)
    gi = lax.broadcasted_iota(jnp.int32, (16, rows), 0)
    named = jnp.zeros((16, rows), F32)
    row = jnp.zeros((16, rows), F32)
    for k in range(3):
        hit = gi == target[k : k + 1]
        named += jnp.where(hit, 1.0, 0.0)
        row += jnp.where(hit, wanted[k : k + 1], 0.0)
    rank = nn(named.astype(BF16), jnp.where(ri < ci, 1.0, 0.0).astype(BF16))
    rank = jnp.where(named > 0.5, rank, -1.0).astype(jnp.int32)
    slot = lax.broadcasted_iota(jnp.int32, (SLOTS, rows), 0)
    lane = lax.broadcasted_iota(jnp.int32, (SLOTS, rows), 1).astype(F32)
    for k in range(16):
        pick = slot == rank[k : k + 1]
        st[k // 4, k % 4] = jnp.where(pick, 1.0, 0.0).astype(BF16)
        slot_row = jnp.max(jnp.where(pick, row[k : k + 1], -1.0), axis=1, keepdims=True)
        rt[k // 4, k % 4] = jnp.where(slot_row == lane, 1.0, 0.0).astype(BF16)

    @pl.when(outer)
    def _():
        def clear(cc, carry):
            col[a(1), cc, :, packed:, :] = jnp.zeros((2, rows - packed, dc), BF16)
            return carry

        lax.fori_loop(0, NC, clear, 0)

    pl.semaphore_wait(barrier, 26 - ((p + 1) // 2) % 2)

    def own(cc):
        load(p_hbm, 0, cc).wait()
        load(q_hbm, 1, cc).wait()
        rcopy(col.at[p, cc], col.at[p, cc], z_s.at[0, cc], col_r.at[p, cc], z_in).start()
        pdst = 2 - 2 * c
        rcopy(col.at[p, cc, 0], bw.at[pdst, cc], own_s.at[0, cc], bw_r.at[pdst, cc], ydev(y - 1 + c, 1 - c)).start()
        qdst = 3 + 2 * c
        rcopy(col.at[p, cc, 1], bw.at[qdst, cc], own_s.at[1, cc], bw_r.at[qdst, cc], ydev(y + c, 1 - c)).start()

    def own_out(cc):
        @pl.when(inner)
        def _():
            for i in range(2):
                ob[cc, i] = nn(pk[i], col[p, cc, i]).astype(BF16)
            rcopy(
                ob.at[cc, :, pl.ds(0, packed)], col.at[p, cc, :, pl.ds(0, packed)],
                z_s.at[1, cc], col_r.at[p, cc], z_out,
            ).start()

    for k in range(AHEAD):
        own(k)

    @pl.when(outer)
    def _():
        for k in range(4):
            rcopy(rt.at[a(1), k], rxo.at[x], ro_s.at[k], ro_r.at[x], xdev(k, a(1))).start()

    for dx in (1, 2, 3):
        xd = (x + dx) % 4
        rcopy(rt.at[:, xd], rx.at[:, x], rx_s.at[dx - 1], rx_r.at[x], xdev(xd, p)).start()
        pd = (p + dx) % 4
        rcopy(st.at[pd], sc.at[p], sc_s.at[dx - 1], sc_r.at[p], xdev(x, pd)).start()
    rx[:, x] = rt[:, x]
    sc[p] = st[p]
    mtx[x, p] = jnp.zeros((SLOTS, rows), BF16)
    acc[...] = jnp.zeros_like(acc)
    wm[...] = jnp.broadcast_to(wrow[...], (rows, rows)).T
    for k in range(4):
        mx[k] = st[:, (x + k) % 4].reshape(rows, rows).astype(F32).T

    unpack = jnp.where((ri % SLOTS < CAP) & (ci == (ri // SLOTS) * CAP + ri % SLOTS), 1.0, 0.0).astype(BF16)

    @pl.when(inner)
    def _():
        for k in range(4):
            got(rxo.at[k], ro_r.at[k])
        pk[0] = tn(unpack, rxo[...].reshape(rows, rows)).astype(BF16)
        pk[1] = tn(unpack, st[a(0)].reshape(rows, rows)).astype(BF16)

    for dx in (1, 2, 3):
        got(rx.at[:, (x + dx) % 4], rx_r.at[(x + dx) % 4])
        got(sc.at[(p + dx) % 4], sc_r.at[(p + dx) % 4])

    @pl.when(outer)
    def _():
        rx[a(1)] = unpack.reshape(4, SLOTS, rows)
        sc[a(1)] = unpack.reshape(4, SLOTS, rows)

    def fwd_col(l, cc, k, dev):
        got(col.at[l, cc], col_r.at[l, cc])
        rcopy(col.at[l, cc], col.at[l, cc], z_s.at[k, cc], col_r.at[l, cc], dev).start()

    def to_win(src, cc, k, dev, hh):
        pi, qi = 1 + 5 * hh, 6 - 2 * hh
        rcopy(src.at[0], bw.at[pi, cc], z_s.at[k, cc], bw_r.at[pi, cc], dev).start()
        rcopy(src.at[1], bw.at[qi, cc], z_s.at[k + 1, cc], bw_r.at[qi, cc], dev).start()

    def hop1(cc):
        @pl.when(outer)
        def _():
            got(col.at[a(2), cc], col_r.at[a(2), cc])
            to_win(col.at[a(2), cc], cc, 5, z_far, 1 - h)

        @pl.when(inner)
        def _():
            fwd_col(a(0), cc, 2, z_in)
            fwd_col(a(2), cc, 3, z_out)

    def hop2(cc):
        @pl.when(inner)
        def _():
            fwd_col(a(3), cc, 4, z_out)

    def hop3(cc):
        @pl.when(outer)
        def _():
            got(col.at[a(3), cc], col_r.at[a(3), cc])
            to_win(col.at[a(3), cc], cc, 3, z_out, 1 - h)

    def win(cc):
        wi = 1 + 3 * h
        got(bw.at[wi, cc], bw_r.at[wi, cc])
        d = h * (5 - 2 * c) + (1 - h) * 2 * c
        rcopy(bw.at[wi, cc], bw.at[d, cc], win_s.at[0, cc], bw_r.at[d, cc], ydev(y, 1 - c)).start()
        got(bw.at[6, cc], bw_r.at[6, cc])
        for c2 in (0, 1):
            d = h * (1 - c2 + c) + (1 - h) * (4 + c2 - c)
            rcopy(
                bw.at[6, cc], bw.at[d, cc], win_s.at[1 + c2, cc], bw_r.at[d, cc], ydev(y + 1 - 2 * h, c2)
            ).start()

    def pick_rows(cc):
        @pl.when(outer)
        def _():
            got(col.at[a(1), cc, :, pl.ds(0, packed)], col_r.at[a(1), cc])

        for l in range(4):
            rows_p = nn(rx[l].reshape(4 * SLOTS, rows), col[l, cc, 0]).astype(BF16)
            xs[:, cc, 0, l * SLOTS : (l + 1) * SLOTS, :] = rows_p.reshape(4, SLOTS, dc)
            rows_q = nn(sc[l].reshape(4 * SLOTS, rows), col[l, cc, 1]).astype(BF16)
            xs[:, cc, 1, l * SLOTS : (l + 1) * SLOTS, :] = rows_q.reshape(4, SLOTS, dc)
        for dx in (2, 1, 3):
            xd = (x + dx) % 4
            rcopy(xs.at[xd, cc], xr.at[x, cc], x_s.at[dx - 1, cc], x_r.at[x, cc], xdev(xd, p)).start()

    def score(cc):
        for i in (0, 2, 3, 5):
            got(bw.at[i, cc], bw_r.at[i, cc])
        got(bw.at[4 - 3 * h, cc], bw_r.at[4 - 3 * h, cc])
        for dx in (1, 2, 3):
            got(xr.at[(x + dx) % 4, cc], x_r.at[(x + dx) % 4, cc])
        q = col[p, cc, 1]
        acc[0] += nt(q, col[p, cc, 0])
        acc[4] += nt(q, xs[x, cc, 0])
        for s in range(3):
            acc[1 + s] += nt(q, bw[s, cc])
            acc[5 + s] += nt(q, xr[(x + 1 + s) % 4, cc, 0])

    def step(t, carry):
        def stage(lag, part):
            @pl.when((t >= lag) & (t < NC + lag))
            def _():
                part(t - lag)

        @pl.when(t + AHEAD < NC)
        def _():
            own(t + AHEAD)

        stage(0, hop1)
        stage(LAG_HOP2, hop2)
        stage(LAG_HOP3, hop3)
        stage(LAG_OUT, own_out)
        stage(LAG_WIN, win)
        stage(LAG_PICK, pick_rows)
        stage(LAG_SCORE, score)
        return carry

    lax.fori_loop(0, NC + LAG_SCORE, step, 0)

    w = wm[...]
    scores = [TEMP * acc[k] for k in range(4)]
    scores += [jnp.where(mx[k] > 0.5, TEMP * acc[4 + k], NEG) for k in range(4)]
    top = scores[0]
    for k in range(1, 8):
        top = jnp.maximum(top, scores[k])
    top = jnp.max(top, axis=1, keepdims=True)
    total = jnp.zeros((rows, rows), F32)
    for k in range(8):
        e = jnp.exp(scores[k] - top)
        total += e if k < 4 else jnp.where(mx[k - 4] > 0.5, e, 0.0)
    log_total = top + jnp.log(jnp.sum(total, axis=1, keepdims=True))
    for k in range(8):
        e = w * jnp.exp(scores[k] - log_total)
        wts[k] = (e if k < 4 else jnp.where(mx[k - 4] > 0.5, e, 0.0)).astype(BF16)
    ones = jnp.ones((rows, rows), BF16)
    for k in range(4):
        by_slot = tn(wts[4 + k], ones)
        want = rt[:, (x + k) % 4].reshape(rows, rows).astype(F32)
        mts[k] = (by_slot * want).astype(BF16).reshape(4, SLOTS, rows)

    for s in range(3):
        rcopy(wts.at[1 + s], wtw.at[s], ww_s.at[s], ww_r.at[s], bdev(1 + s)).start()
        pd = (p + 1 + s) % 4
        rcopy(mts.at[0, pd], mtx.at[x, p], mt_s.at[0, pd], mt_r.at[x, p], xdev(x, pd)).start()
        xd = (x + 1 + s) % 4
        for l in range(4):
            rcopy(mts.at[1 + s, l], mtx.at[x, p], mt_s.at[1 + s, l], mt_r.at[x, p], xdev(xd, l)).start()

    loss[...] = jnp.sum(jnp.where(ri == ci, log_total - scores[0], 0.0), axis=0, keepdims=True)

    def store(src, dst, i, cc):
        return pltpu.make_async_copy(
            src.at[cc], dst.at[:, pl.ds(pl.multiple_of(cc * dc, dc), dc)], st_s.at[i, cc]
        )

    def queries(cc, carry):
        own_p = col[p, cc, 0]
        tot = nn(wts[0], own_p)
        tot += nn(wts[4], xs[x, cc, 0])
        for s in range(3):
            tot += nn(wts[1 + s], bw[s, cc])
            tot += nn(wts[5 + s], xr[(x + 1 + s) % 4, cc, 0])
        oq[cc] = (TEMP * (tot - wm[:, :1] * own_p.astype(F32))).astype(BF16)
        store(oq, gq_hbm, 0, cc).start()
        return carry

    lax.fori_loop(0, NC, queries, 0)

    for s in range(3):
        got(wtw.at[s], ww_r.at[s])
        pd, xd = (p + 1 + s) % 4, (x + 1 + s) % 4
        got(mtx.at[x, pd], mt_r.at[x, pd])
        for l in range(4):
            got(mtx.at[xd, l], mt_r.at[xd, l])

    def passages(cc, carry):
        own_q = col[p, cc, 1]
        tot = tn(wts[0], own_q)
        tot += tn(mtx[x].reshape(rows, rows), xs[x, cc, 1])
        for s in range(3):
            xd = (x + 1 + s) % 4
            tot += tn(wtw[s], bw[3 + s, cc])
            tot += tn(mtx[xd].reshape(rows, rows), xr[xd, cc, 1])
        op[cc] = (TEMP * (tot - wm[:, :1] * own_q.astype(F32))).astype(BF16)
        store(op, gp_hbm, 1, cc).start()
        return carry

    lax.fori_loop(0, NC, passages, 0)

    def drain(cc, carry):
        store(oq, gq_hbm, 0, cc).wait()
        store(op, gp_hbm, 1, cc).wait()
        sent(col.at[p, cc], z_s.at[0, cc])
        sent(col.at[p, cc, 0], own_s.at[0, cc])
        sent(col.at[p, cc, 1], own_s.at[1, cc])
        for k in range(3):
            sent(bw.at[6, cc], win_s.at[k, cc])
            sent(xs.at[0, cc], x_s.at[k, cc])

        @pl.when(outer)
        def _():
            for k in (3, 4, 5, 6):
                sent(col.at[p, cc, 0], z_s.at[k, cc])

        @pl.when(inner)
        def _():
            sent(ob.at[cc, :, pl.ds(0, packed)], z_s.at[1, cc])
            for k in (2, 3, 4):
                sent(col.at[p, cc], z_s.at[k, cc])

        return carry

    lax.fori_loop(0, NC, drain, 0)

    @pl.when(outer)
    def _():
        for k in range(4):
            sent(rt.at[0, 0], ro_s.at[k])

    for s in range(3):
        sent(rt.at[:, 0], rx_s.at[s])
        sent(st.at[0], sc_s.at[s])
        sent(wts.at[1 + s], ww_s.at[s])
        sent(mts.at[0, 0], mt_s.at[0, (p + 1 + s) % 4])
        for l in range(4):
            sent(mts.at[1 + s, l], mt_s.at[1 + s, l])


def per_device(NC, Y, queries, passages, hard_index, weights):
    rows, width = queries.shape
    cap = max(2, (3 * rows + 14) // 15)
    dc = width // NC
    dma = pltpu.SemaphoreType.DMA
    vmem = pl.BlockSpec(memory_space=pltpu.VMEM)
    hbm = pl.BlockSpec(memory_space=pl.ANY)
    loss, gq, gp = pl.pallas_call(
        functools.partial(kernel, NC, Y, cap),
        out_shape=(
            jax.ShapeDtypeStruct((1, rows), F32),
            jax.ShapeDtypeStruct((rows, width), BF16),
            jax.ShapeDtypeStruct((rows, width), BF16),
        ),
        in_specs=[hbm, hbm, vmem, vmem],
        out_specs=(vmem, hbm, hbm),
        scratch_shapes=[
            pltpu.VMEM((4, NC, 2, rows, dc), BF16),
            pltpu.VMEM((7, NC, rows, dc), BF16),
            pltpu.VMEM((4, NC, 2, rows, dc), BF16),
            pltpu.VMEM((4, NC, 2, rows, dc), BF16),
            pltpu.VMEM((NC, 2, rows, dc), BF16),
            pltpu.VMEM((4, 4, SLOTS, rows), BF16),
            pltpu.VMEM((4, 4, SLOTS, rows), BF16),
            pltpu.VMEM((4, 4, SLOTS, rows), BF16),
            pltpu.VMEM((4, 4, SLOTS, rows), BF16),
            pltpu.VMEM((4, SLOTS, rows), BF16),
            pltpu.VMEM((2, rows, rows), BF16),
            pltpu.VMEM((4, rows, rows), F32),
            pltpu.VMEM((rows, rows), F32),
            pltpu.VMEM((8, rows, rows), F32),
            pltpu.VMEM((8, rows, rows), BF16),
            pltpu.VMEM((4, 4, SLOTS, rows), BF16),
            pltpu.VMEM((3, rows, rows), BF16),
            pltpu.VMEM((4, 4, SLOTS, rows), BF16),
            pltpu.VMEM((NC, rows, dc), BF16),
            pltpu.VMEM((NC, rows, dc), BF16),
            dma((2, NC)),
            dma((2, NC)),
            dma((7, NC)),
            dma((4, NC)),
            dma((2, NC)),
            dma((3, NC)),
            dma((7, NC)),
            dma((3, NC)),
            dma((4, NC)),
            dma((3,)), dma((4,)),
            dma((3,)), dma((4,)),
            dma((4,)), dma((4,)),
            dma((3,)), dma((3,)),
            dma((4, 4)), dma((4, 4)),
        ],
        compiler_params=pltpu.CompilerParams(
            collective_id=0, has_side_effects=True, vmem_limit_bytes=60 * 1024 * 1024
        ),
    )(queries, passages, hard_index.T, weights.reshape(1, rows))
    return loss.reshape(rows), gq, gp


def solution(mesh):
    in_specs = (
        P(("grp", "blk"), None),
        P(("grp", "blk"), None),
        P(("grp", "blk"), None),
        P(("grp", "blk")),
    )
    out_specs = (P(("grp", "blk")), P(("grp", "blk"), None), P(("grp", "blk"), None))
    chunks = 16
    return jax.shard_map(
        functools.partial(per_device, chunks, mesh.shape["blk"] // 4),
        mesh=mesh, in_specs=in_specs, out_specs=out_specs, check_vma=False,
    )
```
